32 devices in a mesh: row: 4 (over x, core), col: 8 (over z, y).
Axes of the slice: x: 2, y: 2, z: 4, core: 2. Of those that a mesh axis runs over, the one named last changes fastest.
Arguments:
- pool: bfloat16 [2048, 1024], P(('row', 'col')), may hold values from -16 to 16
- targets: bfloat16 [2048, 1024], P(('row', 'col')), may hold values from -16 to 16
- counts: int32 [2048], P(('row', 'col')), may hold values from 0 to 7, as said below
Outputs:
- proof: float32 [2048], P(('row', 'col'))
- gradient: float32 [2048, 1024], P(('row', 'col'))
The draws below stay inside these ranges and needn't reach their ends.
Inputs may be any that keep to these rules, and one draw needn't show every extreme that they name: `counts`: counts of selections; the last pool example has count 7.
All inputs are finite; a program needn't handle non-finite values.
Results may differ from the reference program's by a relative error of at most 0.0014.
Values may be sent and summed in bfloat16 or wider, within the bound.
A program may use at most 64 MiB of HBM per device.

```python
import math
import jax
import jax.numpy as jnp
from jax import lax

D = 1024
POOL = 2048
TARGETS = 2048


def centre_table(key):
    centre_count = max(POOL // 32, 4)
    base = jax.random.fold_in(key, 9001)
    key_common, key_level, key_spread, key_own = jax.random.split(base, 4)
    common = jax.random.truncated_normal(key_common, -4.0, 4.0, (D,), jnp.float32)
    level = jax.random.uniform(key_level, (centre_count,), jnp.float32, -1.5, 1.5)
    spread = jnp.exp(jax.random.uniform(key_spread, (centre_count,), jnp.float32, math.log(0.3), math.log(1.5)))
    own = jax.random.truncated_normal(key_own, -4.0, 4.0, (centre_count, D), jnp.float32) * spread[:, None]
    return level[:, None] * common[None, :] + own


def draw_examples(key, number, choosable, table):
    key_which, key_scale, key_noise = jax.random.split(key, 3)
    which = jax.random.randint(key_which, (number,), 0, choosable, dtype=jnp.int32)
    scale = jnp.exp(jax.random.uniform(key_scale, (number,), jnp.float32, math.log(0.3), math.log(0.8)))
    noise = jax.random.truncated_normal(key_noise, -4.0, 4.0, (number, D), jnp.float32)
    rows = table[which] + noise * scale[:, None]
    return jnp.clip(rows, -16.0, 16.0).astype(jnp.bfloat16)


def draw_pool(key, part):
    table = centre_table(key)
    return draw_examples(jax.random.fold_in(key, 11), POOL, table.shape[0], table)


def draw_targets(key, part):
    table = centre_table(key)
    return draw_examples(jax.random.fold_in(key, 12), TARGETS, table.shape[0] // 2, table)


def draw_counts(key, part):
    position = jnp.arange(POOL, dtype=jnp.int32)
    ceiling = 1 + 7 * position // POOL
    raw = jax.random.randint(key, (POOL,), 0, 8, dtype=jnp.int32)
    capped = jnp.minimum(raw, ceiling)
    return jnp.where(position == POOL - 1, ceiling, capped).astype(jnp.int32)


def setup_inputs(seed: int = 0) -> dict:
    key_list = jax.random.split(jax.random.key(seed), 4)
    pool = draw_pool(jax.random.fold_in(key_list[3], 71), 0)
    targets = draw_targets(jax.random.fold_in(key_list[3], 71), 0)
    counts = draw_counts(jax.random.fold_in(key_list[3], 71), 0)
    return dict(pool=pool, targets=targets, counts=counts)


def kernel_tile(row_panel, row_norms, columns):
    col_float = columns.astype(jnp.float32)
    col_norms = jnp.sum(col_float * col_float, axis=1)
    inner = jnp.dot(row_panel, columns.T, preferred_element_type=jnp.float32)
    squared = row_norms[:, None] + col_norms[None, :] - 2.0 * inner
    return jnp.exp(-squared * (0.5 / D))


def reference(pool, targets, counts):
    weights = counts.astype(jnp.float32)
    weight_total = jnp.sum(weights)
    block_rows = math.gcd(POOL, 256)

    def one_block(index_block):
        row_panel = lax.dynamic_slice_in_dim(pool, (index_block * block_rows).astype(jnp.int32), block_rows, 0)
        row_float = row_panel.astype(jnp.float32)
        row_norms = jnp.sum(row_float * row_float, axis=1)
        pool_kernel = kernel_tile(row_panel, row_norms, pool) * weights[None, :]
        target_kernel = kernel_tile(row_panel, row_norms, targets)
        pool_mass = jnp.sum(pool_kernel, axis=1)
        target_mass = jnp.sum(target_kernel, axis=1)
        pool_pull = jnp.dot(pool_kernel.astype(jnp.bfloat16), pool, preferred_element_type=jnp.float32)
        target_pull = jnp.dot(target_kernel.astype(jnp.bfloat16), targets, preferred_element_type=jnp.float32)
        proof = target_mass / TARGETS - pool_mass / weight_total
        gradient = (target_pull - target_mass[:, None] * row_float) / TARGETS - (pool_pull - pool_mass[:, None] * row_float) / weight_total
        return proof, gradient

    proof, gradient = lax.map(one_block, jnp.arange(POOL // block_rows, dtype=jnp.int32))
    return proof.reshape(POOL), gradient.reshape(POOL, D)
```

```python
import functools

import jax
import jax.numpy as jnp
from jax import lax
from jax.experimental import pallas as pl
from jax.experimental.pallas import tpu as pltpu
from jax.sharding import PartitionSpec as P

MESH = pl.DeviceIdType.MESH


def kernel(
    R, n, chunks,
    pool, targets, counts,
    g_out, p_out,
    rowbuf, colbuf, cnt, kp, kt, mp, mt, rn, acc, gbuf, pbuf, rs1, rp1, sbuf, spbuf, rs2, rp2,
    loc_sem, cnt_s, cnt_r, cnr_s, cnr_r, row_s, row_r, ring_s, ring_r,
    a_s, a_r, ap_s, ap_r, b_s, b_r, bp_s, bp_r,
):
    b, d = pool.shape
    half, pairs = n // 2, R // 2
    rows = R * b
    part = pairs * b
    dc = d // chunks
    target_count = b * R * n
    mr = lax.axis_index("row")
    mc = lax.axis_index("col")
    core = lax.rem(mr, 2)
    pair = lax.div(mr, 2)
    sibling = mr + 1 - 2 * core
    slot = core * pairs + pair

    def place(position):
        upper = lax.div(position, half)
        return 2 * (position + upper * (n - 1 - 2 * position)) + upper

    step_z = lax.div(mc, 2)
    step_y = lax.rem(mc, 2)
    pos = step_z + step_y * (n - 1 - 2 * step_z)

    def at_distance(k):
        return place(lax.rem(pos + k + n, n))

    neighbour = (at_distance(1), at_distance(-1))

    barrier = pltpu.get_barrier_semaphore()
    for k in range(1, n):
        pl.semaphore_signal(
            barrier, inc=1, device_id={"col": lax.rem(mc + k, n)}, device_id_type=MESH
        )
    for k in range(1, R):
        pl.semaphore_signal(
            barrier, inc=1, device_id={"row": lax.rem(mr + k, R)}, device_id_type=MESH
        )
    pl.semaphore_wait(barrier, n - 1 + R - 1)

    sent = []

    def send(src, dst, send_sem, recv_sem, device):
        copy = pltpu.make_async_remote_copy(
            src_ref=src, dst_ref=dst, send_sem=send_sem, recv_sem=recv_sem,
            device_id=device, device_id_type=MESH,
        )
        copy.start()
        sent.append(copy)
        return copy

    mine = (pool, targets)
    ring = {}

    def hop(s, way, t):
        src = mine[t] if s == 0 else colbuf.at[t, s - 1, way]
        dst = colbuf.at[t, s, 0 if s == half - 1 else way]
        ring[s, way, t] = send(
            src, dst, ring_s.at[s, way, t], ring_r.at[s, way, t], {"col": neighbour[way]}
        )

    count_copies = [
        send(
            counts, cnt.at[mr, mc], cnt_s.at[k], cnt_r.at[k], {"col": lax.rem(mc + k, n)}
        )
        for k in range(1, n)
    ]
    for t in range(2):
        for way in range(2):
            if half > 1 or way == t:
                hop(0, way, t)
    row_copies = [
        send(
            pool, rowbuf.at[slot], row_s.at[k], row_r.at[k], {"row": lax.rem(mr + k, R)}
        )
        for k in range(1, R)
    ]
    local = [
        pltpu.make_async_copy(counts, cnt.at[mr, mc], loc_sem.at[0]),
        pltpu.make_async_copy(pool, rowbuf.at[slot], loc_sem.at[1]),
        pltpu.make_async_copy(pool, colbuf.at[0, half - 1, 1], loc_sem.at[2]),
        pltpu.make_async_copy(targets, colbuf.at[1, half - 1, 1], loc_sem.at[3]),
    ]
    for copy in local:
        copy.start()
    local[0].wait()
    for copy in count_copies:
        copy.wait_recv()
    count_rows = [
        send(
            cnt.at[mr], cnt.at[mr], cnr_s.at[k], cnr_r.at[k], {"row": lax.rem(mr + k, R)}
        )
        for k in range(1, R)
    ]
    for copy in local[1:]:
        copy.wait()
    for copy in row_copies:
        copy.wait_recv()

    rc = min(rows, 256)
    per = rc // b

    def each_rows(body):
        if rows == rc:
            body(0)
        else:
            @pl.loop(0, rows // rc)
            def _(i):
                body(i)

    def span(i):
        return pl.ds(pl.multiple_of(i * rc, rc), rc)

    def panel(i):
        return rowbuf[pl.ds(i * per, per)].reshape(rc, d)

    def norms(i):
        x = panel(i).astype(jnp.float32)
        rn[span(i), :] = jnp.sum(x * x, axis=1, keepdims=True)
        mp[span(i), :] = jnp.zeros((rc, 2 * b), jnp.float32)
        mt[span(i), :] = jnp.zeros((rc, 2 * b), jnp.float32)

    each_rows(norms)

    for copy in count_rows:
        copy.wait_recv()
    all_counts = jnp.sum(cnt[...].astype(jnp.float32), axis=(0, 1))
    weight = 1.0 / jnp.sum(all_counts, axis=1, keepdims=True)
    share = 1.0 / target_count

    def tiles(s):
        x = jnp.concatenate([colbuf[t, s].reshape(2 * b, d) for t in range(2)], axis=0)
        xf = x.astype(jnp.float32)
        sums = jnp.sum(xf * xf, axis=1, keepdims=True)
        col_norms = jnp.broadcast_to(sums, (4 * b, 128)).T[0:1, :]
        first = at_distance(-(s + 1))
        second = mc if s == half - 1 else at_distance(s + 1)
        cw = jnp.concatenate([cnt[mr, first], cnt[mr, second]], axis=1).astype(jnp.float32)

        def body(i):
            inner = lax.dot_general(
                panel(i), x, (((1,), (1,)), ((), ())), preferred_element_type=jnp.float32
            )
            squared = rn[span(i), :] + col_norms - 2.0 * inner
            k = jnp.exp(-squared * (0.5 / d))
            pool_kernel = k[:, : 2 * b] * cw
            target_kernel = k[:, 2 * b :]
            mp[span(i), :] += pool_kernel
            mt[span(i), :] += target_kernel
            where = slice(s * 2 * b, (s + 1) * 2 * b)
            kp[span(i), where] = pool_kernel.astype(jnp.bfloat16)
            kt[span(i), where] = target_kernel.astype(jnp.bfloat16)

        each_rows(body)

    def pull(i, lo, hi, c):
        cols = slice(c * dc, (c + 1) * dc)
        inside = slice(lo * 2 * b, hi * 2 * b)
        p = jnp.dot(
            kp[span(i), inside],
            colbuf[0, lo:hi, :, :, cols].reshape((hi - lo) * 2 * b, dc),
            preferred_element_type=jnp.float32,
        )
        t = jnp.dot(
            kt[span(i), inside],
            colbuf[1, lo:hi, :, :, cols].reshape((hi - lo) * 2 * b, dc),
            preferred_element_type=jnp.float32,
        )
        return t * share - p * weight

    for s in range(half):
        for t in range(2):
            for way in range(2):
                if (s, way, t) in ring:
                    ring[s, way, t].wait_recv()
                    if s + 1 < half - 1 or (s + 1 == half - 1 and way == t):
                        hop(s + 1, way, t)
        if s == half - 1:
            break
        tiles(s)
        if s == half - 2:
            for c in range(chunks):
                def partial(i):
                    acc[c, span(i), :] = pull(i, 0, half - 1, c)

                each_rows(partial)
    tiles(half - 1)

    def masses(i):
        target_mass = jnp.sum(mt[span(i), :], axis=1, keepdims=True)
        pool_mass = jnp.sum(mp[span(i), :], axis=1, keepdims=True)
        proof = target_mass * share - pool_mass * weight
        rn[span(i), :] = proof

    each_rows(masses)
    proof_t = jnp.broadcast_to(rn[...], (rows, 128)).T[0:8, :]
    for r in range(R):
        pbuf[r] = proof_t[:, r * b : (r + 1) * b]

    other = 1 - core
    theirs = pl.ds(pl.multiple_of(other * part, part), part)
    own = pl.ds(pl.multiple_of(core * part, part), part)
    first_p = send(
        pbuf.at[pl.ds(other * pairs, pairs)], rp1, ap_s.at[0], ap_r.at[0], {"row": sibling}
    )
    first_g = []
    for c in range(chunks):
        def finish(i):
            cols = slice(c * dc, (c + 1) * dc)
            x = rowbuf[pl.ds(i * per, per), :, cols].reshape(rc, dc).astype(jnp.float32)
            grad = pull(i, half - 1, half, c) - rn[span(i), :] * x
            if half > 1:
                grad = grad + acc[c, span(i), :]
            gbuf[c, span(i), :] = grad

        each_rows(finish)
        first_g.append(
            send(gbuf.at[c, theirs], rs1.at[c], a_s.at[c], a_r.at[c], {"row": sibling})
        )

    first_p.wait_recv()
    spbuf[...] = pbuf[pl.ds(core * pairs, pairs)] + rp1[...]
    partners = [lax.rem(pair + k, pairs) for k in range(1, pairs)]
    second_p = [
        send(
            spbuf.at[partners[k]], rp2.at[k], bp_s.at[k], bp_r.at[k],
            {"row": 2 * partners[k] + core},
        )
        for k in range(pairs - 1)
    ]
    second_g = []
    for c in range(chunks):
        first_g[c].wait_recv()
        sbuf[c] = (gbuf[c, own, :] + rs1[c]).reshape(pairs, b, dc)
        for k in range(pairs - 1):
            second_g.append(
                send(
                    sbuf.at[c, partners[k]], rs2.at[c, k], b_s.at[c, k], b_r.at[c, k],
                    {"row": 2 * partners[k] + core},
                )
            )
    proof = spbuf[pair]
    for k in range(pairs - 1):
        second_p[k].wait_recv()
        proof = proof + rp2[k]
    p_out[...] = proof[0:1, :]
    for c in range(chunks):
        grad = sbuf[c, pair]
        for k in range(pairs - 1):
            second_g[c * (pairs - 1) + k].wait_recv()
            grad = grad + rs2[c, k]
        g_out[:, c * dc : (c + 1) * dc] = grad
    for copy in sent:
        copy.wait_send()


def on_device(R, n, pool, targets, counts):
    b, d = pool.shape
    half, pairs = n // 2, R // 2
    rows = R * b
    chunks = 4
    dc = d // chunks
    f32, bf16 = jnp.float32, jnp.bfloat16
    dma = pltpu.SemaphoreType.DMA
    far = max(pairs - 1, 1)
    vmem = pl.BlockSpec(memory_space=pltpu.VMEM)
    gradient, proof = pl.pallas_call(
        functools.partial(kernel, R, n, chunks),
        out_shape=(
            jax.ShapeDtypeStruct((b, d), f32),
            jax.ShapeDtypeStruct((1, b), f32),
        ),
        in_specs=[pl.BlockSpec(memory_space=pl.ANY)] * 2 + [vmem],
        out_specs=(vmem, vmem),
        scratch_shapes=[
            pltpu.VMEM((R, b, d), bf16),
            pltpu.VMEM((2, half, 2, b, d), bf16),
            pltpu.VMEM((R, n, 1, b), jnp.int32),
            pltpu.VMEM((rows, n * b), bf16),
            pltpu.VMEM((rows, n * b), bf16),
            pltpu.VMEM((rows, 2 * b), f32),
            pltpu.VMEM((rows, 2 * b), f32),
            pltpu.VMEM((rows, 1), f32),
            pltpu.VMEM((chunks, rows, dc), f32),
            pltpu.VMEM((chunks, rows, dc), f32),
            pltpu.VMEM((R, 8, b), f32),
            pltpu.VMEM((chunks, pairs * b, dc), f32),
            pltpu.VMEM((pairs, 8, b), f32),
            pltpu.VMEM((chunks, pairs, b, dc), f32),
            pltpu.VMEM((pairs, 8, b), f32),
            pltpu.VMEM((chunks, far, b, dc), f32),
            pltpu.VMEM((far, 8, b), f32),
            dma((4,)),
            dma((n,)), dma((n,)),
            dma((R,)), dma((R,)),
            dma((R,)), dma((R,)),
            dma((half, 2, 2)), dma((half, 2, 2)),
            dma((chunks,)), dma((chunks,)),
            dma((1,)), dma((1,)),
            dma((chunks, far)), dma((chunks, far)),
            dma((far,)), dma((far,)),
        ],
        compiler_params=pltpu.CompilerParams(collective_id=0, has_side_effects=True),
    )(pool, targets, counts.reshape(1, b))
    return proof.reshape(b), gradient


def solution(mesh):
    in_specs = (P(("row", "col"), None), P(("row", "col"), None), P(("row", "col")))
    out_specs = (P(("row", "col")), P(("row", "col"), None))
    return jax.shard_map(
        functools.partial(on_device, mesh.shape["row"], mesh.shape["col"]),
        mesh=mesh, in_specs=in_specs, out_specs=out_specs, check_vma=False,
    )
```

```python
import functools

import jax
import jax.numpy as jnp
from jax import lax
from jax.experimental import pallas as pl
from jax.experimental.pallas import tpu as pltpu
from jax.sharding import PartitionSpec as P

MESH = pl.DeviceIdType.MESH


def kernel(
    R, n, chunks,
    pool, targets, counts,
    g_out, p_out, rs2, rp2,
    rowbuf, colbuf, cnt, kp, kt, mp, mt, rn, acc, gbuf, pbuf, rs1, rp1, own_g, sbuf, spbuf,
    loc_sem, cnt_s, cnt_r, cnr_s, cnr_r, row_s, row_r, ring_s, ring_r,
    a_s, a_r, ap_s, ap_r, b_s, b_r, bp_s, bp_r,
):
    b, d = pool.shape
    half, pairs = n // 2, R // 2
    rows = R * b
    part = pairs * b
    dc = d // chunks
    target_count = b * R * n
    mr = lax.axis_index("row")
    mc = lax.axis_index("col")
    core = lax.rem(mr, 2)
    pair = lax.div(mr, 2)
    sibling = mr + 1 - 2 * core
    slot = core * pairs + pair

    def place(position):
        upper = lax.div(position, half)
        return 2 * (position + upper * (n - 1 - 2 * position)) + upper

    step_z = lax.div(mc, 2)
    step_y = lax.rem(mc, 2)
    pos = step_z + step_y * (n - 1 - 2 * step_z)

    def at_distance(k):
        return place(lax.rem(pos + k + n, n))

    neighbour = (at_distance(1), at_distance(-1))

    barrier = pltpu.get_barrier_semaphore()
    for way in range(2):
        pl.semaphore_signal(
            barrier, inc=1, device_id={"col": neighbour[way]}, device_id_type=MESH
        )
    for k in range(1, R):
        pl.semaphore_signal(
            barrier, inc=1, device_id={"row": lax.rem(mr + k, R)}, device_id_type=MESH
        )
    pl.semaphore_wait(barrier, 2 + R - 1)

    sent = []

    def send(src, dst, send_sem, recv_sem, device):
        copy = pltpu.make_async_remote_copy(
            src_ref=src, dst_ref=dst, send_sem=send_sem, recv_sem=recv_sem,
            device_id=device, device_id_type=MESH,
        )
        copy.start()
        sent.append(copy)
        return copy

    mine = (pool, targets)
    ring = {}
    last = half - 1

    def slot_of(s, way):
        return n - 1 if s == last else 2 * s + way

    def hop(s, way, t):
        if s == last and way != t:
            return
        src = mine[t] if s == 0 else colbuf.at[t, slot_of(s - 1, way)]
        ring[s, way, t] = send(
            src, colbuf.at[t, slot_of(s, way)],
            ring_s.at[s, way, t], ring_r.at[s, way, t], {"col": neighbour[way]},
        )

    def count_hop(s, way):
        if s == last and way != 0:
            return
        owner = at_distance(-s if way == 0 else s)
        src = counts if s == 0 else cnt.at[mr, owner]
        ring[s, way, 2] = send(
            src, cnt.at[mr, owner],
            cnt_s.at[s, way], cnt_r.at[s, way], {"col": neighbour[way]},
        )

    for way in range(2):
        count_hop(0, way)
    for t in range(2):
        for way in range(2):
            hop(0, way, t)
    row_copies = [
        send(
            pool, rowbuf.at[slot], row_s.at[k], row_r.at[k], {"row": lax.rem(mr + k, R)}
        )
        for k in range(1, R)
    ]
    local = [
        pltpu.make_async_copy(counts, cnt.at[mr, mc], loc_sem.at[0]),
        pltpu.make_async_copy(pool, rowbuf.at[slot], loc_sem.at[1]),
        pltpu.make_async_copy(pool, colbuf.at[0, n - 2], loc_sem.at[2]),
        pltpu.make_async_copy(targets, colbuf.at[1, n - 2], loc_sem.at[3]),
    ]
    for copy in local:
        copy.start()

    def pass_counts(s):
        for way in range(2):
            if (s, way, 2) in ring:
                ring[s, way, 2].wait_recv()
                if s < last:
                    count_hop(s + 1, way)

    pass_counts(0)
    for copy in local:
        copy.wait()
    for copy in row_copies:
        copy.wait_recv()

    rc = min(rows, 256)
    per = rc // b

    def each_rows(body):
        if rows == rc:
            body(0)
        else:
            @pl.loop(0, rows // rc)
            def _(i):
                body(i)

    def span(i):
        return pl.ds(pl.multiple_of(i * rc, rc), rc)

    def panel(i):
        return rowbuf[pl.ds(i * per, per)].reshape(rc, d)

    def norms(i):
        x = panel(i).astype(jnp.float32)
        rn[span(i), :] = jnp.sum(x * x, axis=1, keepdims=True)
        mp[span(i), :] = jnp.zeros((rc, 2 * b), jnp.float32)
        mt[span(i), :] = jnp.zeros((rc, 2 * b), jnp.float32)

    each_rows(norms)

    def tiles(lo, owners, far=False):
        width = len(owners) * b
        x = jnp.concatenate(
            [colbuf[t, lo : lo + len(owners)].reshape(width, d) for t in range(2)], axis=0
        )
        xf = x.astype(jnp.float32)
        sums = jnp.sum(xf * xf, axis=1, keepdims=True)
        col_norms = jnp.broadcast_to(sums, (2 * width, 128)).T[0:1, :]
        cw = jnp.concatenate([cnt[mr, o] for o in owners], axis=1).astype(jnp.float32)

        def body(i):
            inner = lax.dot_general(
                panel(i), x, (((1,), (1,)), ((), ())), preferred_element_type=jnp.float32
            )
            squared = rn[span(i), :] + col_norms - 2.0 * inner
            k = jnp.exp(-squared * (0.5 / d))
            pool_kernel = k[:, :width] * cw
            target_kernel = k[:, width:]
            mp[span(i), :width] += pool_kernel
            mt[span(i), :width] += target_kernel
            where = slice(0, width) if far else slice(lo * b, lo * b + width)
            kp[span(i), where] = pool_kernel.astype(jnp.bfloat16)
            kt[span(i), where] = target_kernel.astype(jnp.bfloat16)

        each_rows(body)

    def pull(i, inside, lo, hi, c):
        cols = slice(c * dc, (c + 1) * dc)
        p = jnp.dot(
            kp[span(i), inside],
            colbuf[0, lo:hi, :, cols].reshape((hi - lo) * b, dc),
            preferred_element_type=jnp.float32,
        )
        t = jnp.dot(
            kt[span(i), inside],
            colbuf[1, lo:hi, :, cols].reshape((hi - lo) * b, dc),
            preferred_element_type=jnp.float32,
        )
        return t, p

    tiles(n - 2, [mc])
    share = 1.0 / target_count
    for s in range(last):
        if s > 0:
            pass_counts(s)
        for t in range(2):
            for way in range(2):
                ring[s, way, t].wait_recv()
                hop(s + 1, way, t)
        tiles(2 * s, [at_distance(-(s + 1)), at_distance(s + 1)])
    pass_counts(last)
    count_rows = [
        send(
            cnt.at[mr], cnt.at[mr], cnr_s.at[k], cnr_r.at[k], {"row": lax.rem(mr + k, R)}
        )
        for k in range(1, R)
    ]
    for copy in count_rows:
        copy.wait_recv()
    all_counts = jnp.sum(cnt[...].astype(jnp.float32), axis=(0, 1))
    weight = 1.0 / jnp.sum(all_counts, axis=1, keepdims=True)
    for c in range(chunks):
        def partial(i):
            t, p = pull(i, slice(0, (n - 1) * b), 0, n - 1, c)
            acc[c, span(i), :] = t * share - p * weight

        each_rows(partial)
    for t in range(2):
        ring[last, t, t].wait_recv()
    tiles(n - 1, [at_distance(half)], far=True)

    def masses(i):
        target_mass = jnp.sum(mt[span(i), :], axis=1, keepdims=True)
        pool_mass = jnp.sum(mp[span(i), :], axis=1, keepdims=True)
        proof = target_mass * share - pool_mass * weight
        rn[span(i), :] = proof

    each_rows(masses)
    proof_t = jnp.broadcast_to(rn[...], (rows, 128)).T[0:1, :]
    for r in range(R):
        pbuf[r] = proof_t[:, r * b : (r + 1) * b]

    other = 1 - core
    theirs = pl.ds(pl.multiple_of(other * part, part), part)
    first_p = send(
        pbuf.at[pl.ds(other * pairs, pairs)], rp1, ap_s.at[0], ap_r.at[0], {"row": sibling}
    )
    first_g = []
    for c in range(chunks):
        def finish(i):
            cols = slice(c * dc, (c + 1) * dc)
            x = rowbuf[pl.ds(i * per, per), :, cols].reshape(rc, dc).astype(jnp.float32)
            t, p = pull(i, slice(0, b), n - 1, n, c)
            gbuf[c, span(i), :] = acc[c, span(i), :] + (
                t * share - p * weight - rn[span(i), :] * x
            )

        each_rows(finish)
        first_g.append(
            send(gbuf.at[c, theirs], rs1.at[c], a_s.at[c], a_r.at[c], {"row": sibling})
        )

    first_p.wait_recv()
    spbuf[...] = pbuf[pl.ds(core * pairs, pairs)] + rp1[...]
    out_copies = [pltpu.make_async_copy(spbuf.at[pair], p_out, loc_sem.at[0])]
    out_copies[0].start()
    partners = [lax.rem(pair + k, pairs) for k in range(1, pairs)]
    arriving = [
        send(
            spbuf.at[partners[k]], rp2.at[k], bp_s.at[k], bp_r.at[k],
            {"row": 2 * partners[k] + core},
        )
        for k in range(pairs - 1)
    ]
    for c in range(chunks):
        cols = slice(c * dc, (c + 1) * dc)
        first_g[c].wait_recv()
        for k in range(pairs - 1):
            at = pl.multiple_of(partners[k] * b, b)
            block = gbuf[c, pl.ds(pl.multiple_of(core * part + at, b), b), :]
            sbuf[c, k] = (block + rs1[c, pl.ds(at, b), :]).astype(sbuf.dtype)
            arriving.append(
                send(
                    sbuf.at[c, k], rs2.at[k, :, cols], b_s.at[c, k], b_r.at[c, k],
                    {"row": 2 * partners[k] + core},
                )
            )
        at = pl.multiple_of(pair * b, b)
        block = gbuf[c, pl.ds(pl.multiple_of(core * part + at, b), b), :]
        own_g[:, cols] = block + rs1[c, pl.ds(at, b), :]
    out_copies.append(pltpu.make_async_copy(own_g, g_out, loc_sem.at[1]))
    out_copies[1].start()
    for copy in arriving:
        copy.wait_recv()
    for copy in sent:
        copy.wait_send()
    for copy in out_copies:
        copy.wait()


def on_device(R, n, pool, targets, counts):
    b, d = pool.shape
    half, pairs = n // 2, R // 2
    rows = R * b
    chunks = 4
    dc = d // chunks
    f32, bf16 = jnp.float32, jnp.bfloat16
    link = f32
    dma = pltpu.SemaphoreType.DMA
    far = pairs - 1
    hbm = pl.BlockSpec(memory_space=pl.ANY)
    own_g, own_p, far_g, far_p = pl.pallas_call(
        functools.partial(kernel, R, n, chunks),
        out_shape=(
            jax.ShapeDtypeStruct((b, d), f32),
            jax.ShapeDtypeStruct((1, b), f32),
            jax.ShapeDtypeStruct((far, b, d), link),
            jax.ShapeDtypeStruct((far, 1, b), f32),
        ),
        in_specs=[hbm, hbm, pl.BlockSpec(memory_space=pltpu.VMEM)],
        out_specs=(hbm, hbm, hbm, hbm),
        scratch_shapes=[
            pltpu.VMEM((R, b, d), bf16),
            pltpu.VMEM((2, n, b, d), bf16),
            pltpu.VMEM((R, n, 1, b), jnp.int32),
            pltpu.VMEM((rows, n * b), bf16),
            pltpu.VMEM((rows, n * b), bf16),
            pltpu.VMEM((rows, 2 * b), f32),
            pltpu.VMEM((rows, 2 * b), f32),
            pltpu.VMEM((rows, 1), f32),
            pltpu.VMEM((chunks, rows, dc), f32),
            pltpu.VMEM((chunks, rows, dc), f32),
            pltpu.VMEM((R, 1, b), f32),
            pltpu.VMEM((chunks, pairs * b, dc), f32),
            pltpu.VMEM((pairs, 1, b), f32),
            pltpu.VMEM((b, d), f32),
            pltpu.VMEM((chunks, far, b, dc), link),
            pltpu.VMEM((pairs, 1, b), f32),
            dma((4,)),
            dma((half, 2)), dma((half, 2)),
            dma((R,)), dma((R,)),
            dma((R,)), dma((R,)),
            dma((half, 2, 2)), dma((half, 2, 2)),
            dma((chunks,)), dma((chunks,)),
            dma((1,)), dma((1,)),
            dma((chunks, far)), dma((chunks, far)),
            dma((far,)), dma((far,)),
        ],
        compiler_params=pltpu.CompilerParams(collective_id=0, has_side_effects=True),
    )(pool, targets, counts.reshape(1, b))
    gradient = own_g
    proof = own_p.reshape(b)
    for k in range(far):
        gradient = gradient + far_g[k].astype(f32)
        proof = proof + far_p[k].reshape(b)
    return proof, gradient


def solution(mesh):
    in_specs = (P(("row", "col"), None), P(("row", "col"), None), P(("row", "col")))
    out_specs = (P(("row", "col")), P(("row", "col"), None))
    return jax.shard_map(
        functools.partial(on_device, mesh.shape["row"], mesh.shape["col"]),
        mesh=mesh, in_specs=in_specs, out_specs=out_specs, check_vma=False,
    )
```

```python
import functools

import jax
import jax.numpy as jnp
from jax import lax
from jax.experimental import pallas as pl
from jax.experimental.pallas import tpu as pltpu
from jax.sharding import PartitionSpec as P

MESH = pl.DeviceIdType.MESH


def kernel(
    R, n, chunks,
    pool, targets, counts,
    g_out, p_out, rs2, rp2,
    rowbuf, colbuf, cnt, kp, kt, mp, mt, rn, acc, gbuf, pbuf, rs1, rp1, own_g, sbuf, spbuf,
    loc_sem, cnt_s, cnt_r, cnr_s, cnr_r, row_s, row_r, ring_s, ring_r,
    a_s, a_r, ap_s, ap_r, b_s, b_r, bp_s, bp_r,
):
    b, d = pool.shape
    half, pairs = n // 2, R // 2
    rows = R * b
    part = pairs * b
    dc = d // chunks
    target_count = b * R * n
    mr = lax.axis_index("row")
    mc = lax.axis_index("col")
    core = lax.rem(mr, 2)
    pair = lax.div(mr, 2)
    sibling = mr + 1 - 2 * core
    slot = core * pairs + pair

    def place(position):
        upper = lax.div(position, half)
        return 2 * (position + upper * (n - 1 - 2 * position)) + upper

    step_z = lax.div(mc, 2)
    step_y = lax.rem(mc, 2)
    pos = step_z + step_y * (n - 1 - 2 * step_z)

    def at_distance(k):
        return place(lax.rem(pos + k + n, n))

    neighbour = (at_distance(1), at_distance(-1))

    barrier = pltpu.get_barrier_semaphore()
    for way in range(2):
        pl.semaphore_signal(
            barrier, inc=1, device_id={"col": neighbour[way]}, device_id_type=MESH
        )
    for k in range(1, R):
        pl.semaphore_signal(
            barrier, inc=1, device_id={"row": lax.rem(mr + k, R)}, device_id_type=MESH
        )
    pl.semaphore_wait(barrier, 2 + R - 1)

    sent = []

    def send(src, dst, send_sem, recv_sem, device):
        copy = pltpu.make_async_remote_copy(
            src_ref=src, dst_ref=dst, send_sem=send_sem, recv_sem=recv_sem,
            device_id=device, device_id_type=MESH,
        )
        copy.start()
        sent.append(copy)
        return copy

    mine = (pool, targets)
    ring = {}
    last = half - 1

    def slot_of(s, way):
        return n - 1 if s == last else 2 * s + way

    def hop(s, way, t):
        if s == last and way != t:
            return
        src = mine[t] if s == 0 else colbuf.at[t, slot_of(s - 1, way)]
        ring[s, way, t] = send(
            src, colbuf.at[t, slot_of(s, way)],
            ring_s.at[s, way, t], ring_r.at[s, way, t], {"col": neighbour[way]},
        )

    def count_hop(s, way):
        if s == last and way != 0:
            return
        owner = at_distance(-s if way == 0 else s)
        src = counts if s == 0 else cnt.at[mr, owner]
        ring[s, way, 2] = send(
            src, cnt.at[mr, owner],
            cnt_s.at[s, way], cnt_r.at[s, way], {"col": neighbour[way]},
        )

    for way in range(2):
        count_hop(0, way)
    for way in range(2):
        hop(0, way, 0)
    row_copies = [
        send(
            pool, rowbuf.at[slot], row_s.at[k], row_r.at[k], {"row": lax.rem(mr + k, R)}
        )
        for k in range(1, R)
    ]
    local = [
        pltpu.make_async_copy(counts, cnt.at[mr, mc], loc_sem.at[0]),
        pltpu.make_async_copy(pool, rowbuf.at[slot], loc_sem.at[1]),
        pltpu.make_async_copy(pool, colbuf.at[0, n - 2], loc_sem.at[2]),
        pltpu.make_async_copy(targets, colbuf.at[1, n - 2], loc_sem.at[3]),
    ]
    for copy in local:
        copy.start()

    def pass_counts(s):
        for way in range(2):
            if (s, way, 2) in ring:
                ring[s, way, 2].wait_recv()
                if s < last:
                    count_hop(s + 1, way)

    for way in range(2):
        ring[0, way, 0].wait_send()
        sent[:] = [c for c in sent if c is not ring[0, way, 0]]
    for way in range(2):
        hop(0, way, 1)
    pass_counts(0)
    for copy in local:
        copy.wait()
    for copy in row_copies:
        copy.wait_recv()

    rc = min(rows, 256)
    per = rc // b

    def each_rows(body):
        if rows == rc:
            body(0)
        else:
            @pl.loop(0, rows // rc)
            def _(i):
                body(i)

    def span(i):
        return pl.ds(pl.multiple_of(i * rc, rc), rc)

    def panel(i):
        return rowbuf[pl.ds(i * per, per)].reshape(rc, d)

    def norms(i):
        x = panel(i).astype(jnp.float32)
        rn[span(i), :] = jnp.sum(x * x, axis=1, keepdims=True)
        mp[span(i), :] = jnp.zeros((rc, 2 * b), jnp.float32)
        mt[span(i), :] = jnp.zeros((rc, 2 * b), jnp.float32)

    each_rows(norms)

    def tiles(lo, owners, far=False):
        width = len(owners) * b
        x = jnp.concatenate(
            [colbuf[t, lo : lo + len(owners)].reshape(width, d) for t in range(2)], axis=0
        )
        xf = x.astype(jnp.float32)
        sums = jnp.sum(xf * xf, axis=1, keepdims=True)
        col_norms = jnp.broadcast_to(sums, (2 * width, 128)).T[0:1, :]
        cw = jnp.concatenate([cnt[mr, o] for o in owners], axis=1).astype(jnp.float32)

        def body(i):
            inner = lax.dot_general(
                panel(i), x, (((1,), (1,)), ((), ())), preferred_element_type=jnp.float32
            )
            squared = rn[span(i), :] + col_norms - 2.0 * inner
            k = jnp.exp(-squared * (0.5 / d))
            pool_kernel = k[:, :width] * cw
            target_kernel = k[:, width:]
            mp[span(i), :width] += pool_kernel
            mt[span(i), :width] += target_kernel
            where = slice(0, width) if far else slice(lo * b, lo * b + width)
            kp[span(i), where] = pool_kernel.astype(jnp.bfloat16)
            kt[span(i), where] = target_kernel.astype(jnp.bfloat16)

        each_rows(body)

    def pull(i, inside, lo, hi, c):
        cols = slice(c * dc, (c + 1) * dc)
        p = jnp.dot(
            kp[span(i), inside],
            colbuf[0, lo:hi, :, cols].reshape((hi - lo) * b, dc),
            preferred_element_type=jnp.float32,
        )
        t = jnp.dot(
            kt[span(i), inside],
            colbuf[1, lo:hi, :, cols].reshape((hi - lo) * b, dc),
            preferred_element_type=jnp.float32,
        )
        return t, p

    tiles(n - 2, [mc])
    share = 1.0 / target_count
    for s in range(last):
        if s > 0:
            pass_counts(s)
        for t in range(2):
            for way in range(2):
                ring[s, way, t].wait_recv()
                hop(s + 1, way, t)
        tiles(2 * s, [at_distance(-(s + 1)), at_distance(s + 1)])
    pass_counts(last)
    count_rows = [
        send(
            cnt.at[mr], cnt.at[mr], cnr_s.at[k], cnr_r.at[k], {"row": lax.rem(mr + k, R)}
        )
        for k in range(1, R)
    ]
    for copy in count_rows:
        copy.wait_recv()
    all_counts = jnp.sum(cnt[...].astype(jnp.float32), axis=(0, 1))
    weight = 1.0 / jnp.sum(all_counts, axis=1, keepdims=True)
    for c in range(chunks):
        def partial(i):
            t, p = pull(i, slice(0, (n - 1) * b), 0, n - 1, c)
            acc[c, span(i), :] = t * share - p * weight

        each_rows(partial)
    for t in range(2):
        ring[last, t, t].wait_recv()
    tiles(n - 1, [at_distance(half)], far=True)

    def masses(i):
        target_mass = jnp.sum(mt[span(i), :], axis=1, keepdims=True)
        pool_mass = jnp.sum(mp[span(i), :], axis=1, keepdims=True)
        proof = target_mass * share - pool_mass * weight
        rn[span(i), :] = proof

    each_rows(masses)
    proof_t = jnp.broadcast_to(rn[...], (rows, 128)).T[0:1, :]
    for r in range(R):
        pbuf[r] = proof_t[:, r * b : (r + 1) * b]

    other = 1 - core
    theirs = pl.ds(pl.multiple_of(other * part, part), part)
    first_p = send(
        pbuf.at[pl.ds(other * pairs, pairs)], rp1, ap_s.at[0], ap_r.at[0], {"row": sibling}
    )
    first_g = []
    for c in range(chunks):
        def finish(i):
            cols = slice(c * dc, (c + 1) * dc)
            x = rowbuf[pl.ds(i * per, per), :, cols].reshape(rc, dc).astype(jnp.float32)
            t, p = pull(i, slice(0, b), n - 1, n, c)
            gbuf[c, span(i), :] = acc[c, span(i), :] + (
                t * share - p * weight - rn[span(i), :] * x
            )

        each_rows(finish)
        first_g.append(
            send(gbuf.at[c, theirs], rs1.at[c], a_s.at[c], a_r.at[c], {"row": sibling})
        )

    first_p.wait_recv()
    spbuf[...] = pbuf[pl.ds(core * pairs, pairs)] + rp1[...]
    out_copies = [pltpu.make_async_copy(spbuf.at[pair], p_out, loc_sem.at[0])]
    out_copies[0].start()
    partners = [lax.rem(pair + k, pairs) for k in range(1, pairs)]
    arriving = [
        send(
            spbuf.at[partners[k]], rp2.at[k], bp_s.at[k], bp_r.at[k],
            {"row": 2 * partners[k] + core},
        )
        for k in range(pairs - 1)
    ]
    for c in range(chunks):
        cols = slice(c * dc, (c + 1) * dc)
        first_g[c].wait_recv()
        for k in range(pairs - 1):
            at = pl.multiple_of(partners[k] * b, b)
            block = gbuf[c, pl.ds(pl.multiple_of(core * part + at, b), b), :]
            sbuf[c, k] = (block + rs1[c, pl.ds(at, b), :]).astype(sbuf.dtype)
            arriving.append(
                send(
                    sbuf.at[c, k], rs2.at[k, :, cols], b_s.at[c, k], b_r.at[c, k],
                    {"row": 2 * partners[k] + core},
                )
            )
        at = pl.multiple_of(pair * b, b)
        block = gbuf[c, pl.ds(pl.multiple_of(core * part + at, b), b), :]
        own_g[:, cols] = block + rs1[c, pl.ds(at, b), :]
    out_copies.append(pltpu.make_async_copy(own_g, g_out, loc_sem.at[1]))
    out_copies[1].start()
    for copy in arriving:
        copy.wait_recv()
    for copy in sent:
        copy.wait_send()
    for copy in out_copies:
        copy.wait()


def on_device(R, n, pool, targets, counts):
    b, d = pool.shape
    half, pairs = n // 2, R // 2
    rows = R * b
    chunks = 4
    dc = d // chunks
    f32, bf16 = jnp.float32, jnp.bfloat16
    link = f32
    dma = pltpu.SemaphoreType.DMA
    far = pairs - 1
    hbm = pl.BlockSpec(memory_space=pl.ANY)
    own_g, own_p, far_g, far_p = pl.pallas_call(
        functools.partial(kernel, R, n, chunks),
        out_shape=(
            jax.ShapeDtypeStruct((b, d), f32),
            jax.ShapeDtypeStruct((1, b), f32),
            jax.ShapeDtypeStruct((far, b, d), link),
            jax.ShapeDtypeStruct((far, 1, b), f32),
        ),
        in_specs=[pl.BlockSpec(memory_space=pltpu.HBM)] * 2 + [pl.BlockSpec(memory_space=pltpu.VMEM)],
        out_specs=(hbm, hbm, hbm, hbm),
        scratch_shapes=[
            pltpu.VMEM((R, b, d), bf16),
            pltpu.VMEM((2, n, b, d), bf16),
            pltpu.VMEM((R, n, 1, b), jnp.int32),
            pltpu.VMEM((rows, n * b), bf16),
            pltpu.VMEM((rows, n * b), bf16),
            pltpu.VMEM((rows, 2 * b), f32),
            pltpu.VMEM((rows, 2 * b), f32),
            pltpu.VMEM((rows, 1), f32),
            pltpu.VMEM((chunks, rows, dc), f32),
            pltpu.VMEM((chunks, rows, dc), f32),
            pltpu.VMEM((R, 1, b), f32),
            pltpu.VMEM((chunks, pairs * b, dc), f32),
            pltpu.VMEM((pairs, 1, b), f32),
            pltpu.VMEM((b, d), f32),
            pltpu.VMEM((chunks, far, b, dc), link),
            pltpu.VMEM((pairs, 1, b), f32),
            dma((4,)),
            dma((half, 2)), dma((half, 2)),
            dma((R,)), dma((R,)),
            dma((R,)), dma((R,)),
            dma((half, 2, 2)), dma((half, 2, 2)),
            dma((chunks,)), dma((chunks,)),
            dma((1,)), dma((1,)),
            dma((chunks, far)), dma((chunks, far)),
            dma((far,)), dma((far,)),
        ],
        compiler_params=pltpu.CompilerParams(vmem_limit_bytes=(16 << 20) + 32 * rows * d, collective_id=0, has_side_effects=True),
    )(pool, targets, counts.reshape(1, b))
    gradient = own_g
    proof = own_p.reshape(b)
    for k in range(far):
        gradient = gradient + far_g[k].astype(f32)
        proof = proof + far_p[k].reshape(b)
    return proof, gradient


def solution(mesh):
    in_specs = (P(("row", "col"), None), P(("row", "col"), None), P(("row", "col")))
    out_specs = (P(("row", "col")), P(("row", "col"), None))
    return jax.shard_map(
        functools.partial(on_device, mesh.shape["row"], mesh.shape["col"]),
        mesh=mesh, in_specs=in_specs, out_specs=out_specs, check_vma=False,
    )
```
